32 devices in a mesh: dp: 4 (over x, core), seq: 8 (over z, y).
Axes of the slice: x: 2, y: 2, z: 4, core: 2. Of those that a mesh axis runs over, the one named last changes fastest.
Arguments:
- q_raw: bfloat16 [4, 1024, 4096], P('dp', 'seq'), may hold values from -64 to 64
- k_raw: bfloat16 [4, 1024, 4096], P('dp', 'seq'), may hold values from -64 to 64
- values: bfloat16 [4, 1024, 4096], P('dp', 'seq'), may hold values from -6 to 6
- grad_out: bfloat16 [4, 1024, 4096], P('dp', 'seq'), may hold values from -6 to 6
- q_gain: float32 [4096], replicated, may hold values from 0.1 to 1.9
- k_gain: float32 [4096], replicated, may hold values from 0.1 to 1.9
- lengths: int32 [4, 6], P('dp'), may hold values from 1 to 341, 1024 in all within a row
- positions: int32 [4, 3, 1024], P('dp', None, 'seq'), may hold values from 0 to 63
Outputs:
- attended: bfloat16 [4, 1024, 4096], P('dp', 'seq')
- grad_q: bfloat16 [4, 1024, 4096], P('dp', 'seq')
- grad_k: bfloat16 [4, 1024, 4096], P('dp', 'seq')
- grad_v: bfloat16 [4, 1024, 4096], P('dp', 'seq')
- grad_q_gain: float32 [4096], replicated
- grad_k_gain: float32 [4096], replicated
The draws below stay inside these ranges and needn't reach their ends.
Inputs may be any that keep to these rules, and one draw needn't show every extreme that they name: `lengths`: the clips of a bucket lie end to end and fill its 1024 tokens.
All inputs are finite; a program needn't handle non-finite values.
Results may differ from the reference program's by a relative error of at most 0.012.
The reference program's roundings to bfloat16 on the way (of `weights`, `prob_half` and `dscore`) count: a program that leaves them out, or rounds other values in their place, can miss the bound.
Values may be sent and summed in bfloat16 or wider, within the bound.
A program may use at most 128 MiB of HBM per device.

```python
import math
import jax
import jax.numpy as jnp
import numpy as np
from jax import lax

HEADS = 32
HEAD_DIM = 128
FEAT = 4096
TOKENS = 1024
CLIPS = 6
CLIP_MOST = 341
GRID = 64
N_DP = 4


def draw_pair(key):
    base = jax.random.fold_in(key, 11)
    shape = (N_DP, TOKENS, FEAT)
    query = jax.random.normal(jax.random.fold_in(base, 1), shape, jnp.float32)
    keys = jax.random.normal(jax.random.fold_in(base, 2), shape, jnp.float32)
    return (jnp.clip(query, -64.0, 64.0), jnp.clip(keys, -64.0, 64.0))


def draw_q_raw(key, part):
    return draw_pair(key)[0].astype(jnp.bfloat16)


def draw_k_raw(key, part):
    return draw_pair(key)[1].astype(jnp.bfloat16)


def plant(array, rng, least, top_value):
    place = [jax.random.randint(jax.random.fold_in(rng, axis), (), 0, length) for axis, length in enumerate(array.shape)]
    main_axis = array.shape.index(max(array.shape))
    beside = place[:main_axis] + [(place[main_axis] + 1) % array.shape[main_axis]] + place[main_axis + 1:]
    return array.at[tuple(place)].set(least).at[tuple(beside)].set(top_value)


def block_scale(rng, extent, pieces, least, top_value):
    factor_of, own = 1.0, jax.random.fold_in(rng, 6)
    for axis_at, parts in pieces:
        draws = jnp.exp(jax.random.uniform(jax.random.fold_in(own, axis_at), (parts,), jnp.float32, least / len(pieces), top_value / len(pieces)))
        factor_of = factor_of * jnp.repeat(draws, extent[axis_at] // parts).reshape([-1 if axis == axis_at else 1 for axis in range(len(extent))])
    return factor_of


def length_profile(amount, total, most, skew):
    weights = [(1 << 20) // math.isqrt(standing ** skew) + 1 for standing in range(2, amount + 1)]
    surplus, counts = total - most - (amount - 1), [1] * (amount - 1)
    while surplus > 0:
        free = [i for i in range(amount - 1) if counts[i] < most]
        pool, budget = sum([weights[i] for i in free]), surplus
        for i in free:
            extra = min(most - counts[i], max(1, budget * weights[i] // pool), surplus)
            counts[i] = counts[i] + extra
            surplus = surplus - extra
    return np.array([most] + counts)


def ragged(rng, number_of, total, most, skew):
    if number_of == 2:
        one = jax.random.randint(rng, (), max(1, total - most), min(most, total - 1) + 1)
        return jnp.stack([one, total - one])
    sizes = jnp.asarray(length_profile(number_of, total, most, skew), jnp.int32)
    pairs = (number_of - 1) // 2
    source_of, sink = sizes[1:1 + 2 * pairs:2], sizes[2:2 + 2 * pairs:2]
    slack = jnp.minimum(source_of - 1, most - sink)
    moved = jax.random.randint(jax.random.fold_in(rng, 1), (pairs,), 0, 1 << 20) % (slack + 1)
    sizes = sizes.at[1:1 + 2 * pairs:2].set(source_of - moved).at[2:2 + 2 * pairs:2].set(sink + moved)
    return sizes[jax.random.permutation(jax.random.fold_in(rng, 2), number_of)]


def noise(own_key, shape, scale, limit, shards=(), held_as=jnp.bfloat16):
    factor_of = block_scale(own_key, shape, shards, -0.22, 0.18) if shards else 1.0
    entries = jax.random.normal(own_key, shape, jnp.float32) * scale * factor_of
    return jnp.minimum(jnp.maximum(entries, -limit), limit).astype(held_as)


def setup_inputs(seed: int = 0) -> dict:
    arg_keys = jax.random.split(jax.random.key(seed), 9)
    q_raw = draw_q_raw(jax.random.fold_in(arg_keys[8], 71), 0)
    k_raw = draw_k_raw(jax.random.fold_in(arg_keys[8], 71), 0)
    values = noise(arg_keys[2], (N_DP, TOKENS, FEAT), 1.0, 6.0, ((0, 4), (1, 8)))
    grad_out = noise(arg_keys[3], (N_DP, TOKENS, FEAT), 1.0, 6.0, ((0, 4), (1, 8)))
    q_gain = jnp.clip(1.0 + 0.18 * jax.random.normal(arg_keys[4], (FEAT,), jnp.float32), 0.1, 1.9)
    k_gain = jnp.clip(1.0 + 0.18 * jax.random.normal(arg_keys[5], (FEAT,), jnp.float32), 0.1, 1.9)
    lengths = jax.vmap(lambda own: ragged(own, CLIPS, TOKENS, CLIP_MOST, 2))(jax.random.split(arg_keys[6], N_DP)).reshape((N_DP, CLIPS)).astype(jnp.int32)
    positions = plant(jax.random.randint(arg_keys[7], (N_DP, 3, TOKENS), 0, GRID), jax.random.fold_in(arg_keys[7], 1), 0, GRID - 1).astype(jnp.int32)
    return {"q_raw": q_raw, "k_raw": k_raw, "values": values, "grad_out": grad_out, "q_gain": q_gain, "k_gain": k_gain, "lengths": lengths, "positions": positions}


epsilon = 1e-06

def product(form, left, right):
    return jnp.einsum(form, left.astype(jnp.float32), right.astype(jnp.float32))

def segment_ids(clip_lengths, tokens):
    boundary = jnp.cumsum(clip_lengths).astype(jnp.int32)
    places = jnp.arange(tokens, dtype=jnp.int32)
    return lax.optimization_barrier(jnp.sum((boundary[None, :] <= places[:, None]).astype(jnp.int32), axis=1)).astype(jnp.int32)

def rope_tables(position_rows, head_dim):
    half = head_dim // 2
    sixth = head_dim // 6
    first = half - 2 * sixth
    pairs = jnp.arange(half, dtype=jnp.int32)
    section = (pairs >= first).astype(jnp.int32) + (pairs >= first + sixth).astype(jnp.int32)
    begin = jnp.where(section == 0, 0, jnp.where(section == 1, first, first + sixth))
    number = jnp.where(section == 0, first, sixth)
    freqs = 10000.0 ** (-(pairs - begin).astype(jnp.float32) / number.astype(jnp.float32))
    picker = (section[None, :] == jnp.arange(3, dtype=jnp.int32)[:, None]).astype(jnp.float32) * freqs[None, :]
    angle = lax.dot_general(position_rows.astype(jnp.float32), picker, (((0,), (0,)), ((), ())), precision=lax.Precision.HIGHEST)
    cosine = jnp.cos(angle)
    sine = jnp.sin(angle)
    return (jnp.concatenate([cosine, cosine], axis=-1), jnp.concatenate([sine, sine], axis=-1))

def rotate_pairs(inputs, cosine, sine):
    half = inputs.shape[-1] // 2
    partner = jnp.concatenate([-inputs[..., half:], inputs[..., :half]], axis=-1)
    return inputs * cosine[:, None, :] + partner * sine[:, None, :]

def rotate_back(grads, cosine, sine):
    half = grads.shape[-1] // 2
    turned = grads * sine[:, None, :]
    return grads * cosine[:, None, :] + jnp.concatenate([turned[..., half:], -turned[..., :half]], axis=-1)

def attention_forward(query, keys, value_rows, segment, block, window, reach):
    count = query.shape[0]
    scale = query.shape[2] ** (-0.5)

    def one_block(index_block):
        start = (index_block * block).astype(jnp.int32)
        key_start = jnp.clip(start - reach, 0, count - window).astype(jnp.int32)
        query_block = lax.dynamic_slice_in_dim(query, start, block, 0)
        key_window = lax.dynamic_slice_in_dim(keys, key_start, window, 0)
        value_window = lax.dynamic_slice_in_dim(value_rows, key_start, window, 0)
        query_clip = lax.dynamic_slice_in_dim(segment, start, block, 0)
        key_clip = lax.dynamic_slice_in_dim(segment, key_start, window, 0)
        scores = product('qhd,khd->hqk', query_block, key_window) * scale
        live = (query_clip[:, None] == key_clip[None, :])[None]
        scores = jnp.where(live, scores, -1e+30)
        highest = lax.optimization_barrier(jnp.max(scores, axis=-1, keepdims=True))
        expon = jnp.exp(scores - highest)
        totals = lax.optimization_barrier(jnp.sum(expon, axis=-1, keepdims=True))
        weights = (expon / totals).astype(jnp.bfloat16)
        output = product('hqk,khd->qhd', weights, value_window)
        return (output, (highest + jnp.log(totals))[..., 0])
    outputs, logsum = lax.map(one_block, jnp.arange(count // block, dtype=jnp.int32))
    return (outputs.reshape(query.shape), logsum)

def attention_backward(query, keys, value_rows, context, cotangent, logsum, segment, block, window, reach):
    count = query.shape[0]
    scale = query.shape[2] ** (-0.5)
    delta = lax.optimization_barrier(jnp.sum(cotangent.astype(jnp.float32) * context.astype(jnp.float32), axis=-1))

    def one_block(carry, inputs):
        key_acc, value_acc = carry
        index_block, block_logsum = inputs
        start = (index_block * block).astype(jnp.int32)
        key_start = jnp.clip(start - reach, 0, count - window).astype(jnp.int32)
        query_block = lax.dynamic_slice_in_dim(query, start, block, 0)
        cot_block = lax.dynamic_slice_in_dim(cotangent, start, block, 0)
        delta_block = lax.dynamic_slice_in_dim(delta, start, block, 0)
        key_window = lax.dynamic_slice_in_dim(keys, key_start, window, 0)
        value_window = lax.dynamic_slice_in_dim(value_rows, key_start, window, 0)
        query_clip = lax.dynamic_slice_in_dim(segment, start, block, 0)
        key_clip = lax.dynamic_slice_in_dim(segment, key_start, window, 0)
        scores = product('qhd,khd->hqk', query_block, key_window) * scale
        live = (query_clip[:, None] == key_clip[None, :])[None]
        probs = jnp.where(live, jnp.exp(scores - block_logsum[:, :, None]), 0.0)
        prob_half = probs.astype(jnp.bfloat16)
        value_grad = product('hqk,qhd->khd', prob_half, cot_block)
        dprob = product('qhd,khd->hqk', cot_block, value_window)
        dscore = (probs * (dprob - jnp.transpose(delta_block)[:, :, None]) * scale).astype(jnp.bfloat16)
        query_grad = product('hqk,khd->qhd', dscore, key_window)
        key_grad = product('hqk,qhd->khd', dscore, query_block)
        key_acc = lax.dynamic_update_slice_in_dim(key_acc, lax.dynamic_slice_in_dim(key_acc, key_start, window, 0) + key_grad, key_start, 0)
        value_acc = lax.dynamic_update_slice_in_dim(value_acc, lax.dynamic_slice_in_dim(value_acc, key_start, window, 0) + value_grad, key_start, 0)
        return ((key_acc, value_acc), query_grad)
    zeros = jnp.zeros(query.shape, jnp.float32)
    indices = jnp.arange(count // block, dtype=jnp.int32)
    (key_acc, value_acc), query_grads = lax.scan(one_block, (zeros, zeros), (indices, logsum))
    return (query_grads.reshape(query.shape), key_acc, value_acc)

def norm_backward(grads_half, cosine, sine, scale_rows, hat_rows, gain_row):
    tokens = hat_rows.shape[0]
    grads = lax.optimization_barrier(grads_half).astype(jnp.float32)
    turned = rotate_back(grads, cosine, sine).reshape(tokens, -1)
    gain_part = lax.optimization_barrier(jnp.sum(turned * hat_rows, axis=0))
    lifted = turned * gain_row
    inner = lax.optimization_barrier(jnp.mean(lifted * hat_rows, axis=-1, keepdims=True))
    return ((scale_rows[:, None] * (lifted - hat_rows * inner)).astype(jnp.bfloat16), gain_part)

def reference(q_raw, k_raw, values, grad_out, q_gain, k_gain, lengths, positions):
    reach = CLIP_MOST
    block = min(512, TOKENS)
    window = min(TOKENS, block + 2 * reach)

    def replica(inputs):
        query_raw, key_raw, value_rows, cot_rows, clip_lengths, position_rows = inputs
        segment = segment_ids(clip_lengths, TOKENS)
        cosine, sine = rope_tables(position_rows, HEAD_DIM)
        query_float = query_raw.astype(jnp.float32)
        key_float = key_raw.astype(jnp.float32)
        query_scale = lax.rsqrt(lax.optimization_barrier(jnp.mean(query_float * query_float, axis=-1)) + epsilon)
        key_scale = lax.rsqrt(lax.optimization_barrier(jnp.mean(key_float * key_float, axis=-1)) + epsilon)
        query_hat = query_float * query_scale[:, None]
        key_hat = key_float * key_scale[:, None]
        query_rot = rotate_pairs((query_hat * q_gain).reshape(TOKENS, HEADS, HEAD_DIM), cosine, sine).astype(jnp.bfloat16)
        key_rot = rotate_pairs((key_hat * k_gain).reshape(TOKENS, HEADS, HEAD_DIM), cosine, sine).astype(jnp.bfloat16)
        value_heads = value_rows.reshape(TOKENS, HEADS, HEAD_DIM)
        context, logsum = attention_forward(query_rot, key_rot, value_heads, segment, block, window, reach)
        context_half = context.astype(jnp.bfloat16)
        cot_heads = cot_rows.reshape(TOKENS, HEADS, HEAD_DIM)
        query_grad, key_grad, value_grad = attention_backward(query_rot, key_rot, value_heads, context_half, cot_heads, logsum, segment, block, window, reach)
        query_input, query_part = norm_backward(query_grad.astype(jnp.bfloat16), cosine, sine, query_scale, query_hat, q_gain)
        key_input, key_part = norm_backward(key_grad.astype(jnp.bfloat16), cosine, sine, key_scale, key_hat, k_gain)
        return (context_half.reshape(TOKENS, FEAT), query_input, key_input, value_grad.astype(jnp.bfloat16).reshape(TOKENS, FEAT), query_part, key_part)
    attended, grad_q, grad_k, grad_v, query_parts, key_parts = lax.map(replica, (q_raw, k_raw, values, grad_out, lengths, positions))
    return (attended, grad_q, grad_k, grad_v, lax.optimization_barrier(jnp.sum(query_parts, axis=0)) / N_DP, lax.optimization_barrier(jnp.sum(key_parts, axis=0)) / N_DP)
```

```python
import functools

import jax
import jax.numpy as jnp
import numpy as np
from jax import lax
from jax.experimental import pallas as pl
from jax.experimental.pallas import tpu as pltpu
from jax.sharding import PartitionSpec as P

HEAD_DIM = 128
LANES = 128
QUERY_BLOCK = 256
EPSILON = 1e-06
MESH = pl.DeviceIdType.MESH


def rope_tables(position_rows, head_dim):
    half = head_dim // 2
    sixth = head_dim // 6
    first = half - 2 * sixth
    pairs = np.arange(head_dim) % half
    section = (pairs >= first).astype(np.int32) + (pairs >= first + sixth).astype(np.int32)
    begin = np.where(section == 0, 0, np.where(section == 1, first, first + sixth))
    number = np.where(section == 0, first, sixth)
    freqs = (10000.0 ** (-(pairs - begin) / number)).astype(np.float32)
    sign = np.where(np.arange(head_dim) < half, -1.0, 1.0).astype(np.float32)
    rows = position_rows.astype(jnp.float32)[:, :, None]
    chosen = jnp.where(section == 0, rows[0], jnp.where(section == 1, rows[1], rows[2]))
    angle = chosen * freqs
    return jnp.cos(angle), jnp.sin(angle) * sign


def dot(left, right, left_dim, right_dim):
    return lax.dot_general(
        left, right, (((left_dim,), (right_dim,)), ((), ())), preferred_element_type=jnp.float32
    )


def kernel(
    sizes,
    len_ref, q_ref, k_ref, v_ref, do_ref, gq_ref, gk_ref, cos_ref, sin_ref,
    out_ref, gain_ref,
    sent, recv, back, key_acc, value_acc, scale_q, scale_k,
    part, seq_part, dp_sum, dp_part, total,
    in_send, in_recv, own_sem, out_send, out_recv, gain_send, gain_recv,
):
    n, replicas, heads, tok, clips, reach = sizes
    tokens = n * tok
    feature = n * heads * HEAD_DIM
    me = lax.axis_index("seq")
    my_dp = lax.axis_index("dp")
    scale = HEAD_DIM ** (-0.5)

    def peer(step):
        return lax.rem(me + step, n)

    def columns(owner, head):
        return pl.ds(pl.multiple_of((owner * heads + head) * HEAD_DIM, HEAD_DIM), HEAD_DIM)

    def rows(owner):
        return pl.ds(pl.multiple_of(owner * tok, tok), tok)

    def remote(src, dst, send_sem, recv_sem, device):
        return pltpu.make_async_remote_copy(
            src_ref=src, dst_ref=dst, send_sem=send_sem, recv_sem=recv_sem,
            device_id=device, device_id_type=MESH,
        )

    barrier = pltpu.get_barrier_semaphore()
    for step in range(1, n):
        pl.semaphore_signal(barrier, inc=1, device_id=(my_dp, peer(step)), device_id_type=MESH)
    for step in range(1, replicas):
        other = lax.rem(my_dp + step, replicas)
        pl.semaphore_signal(barrier, inc=1, device_id=(other, me), device_id_type=MESH)
    pl.semaphore_wait(barrier, n - 1 + replicas - 1)

    def send_values(head):
        pltpu.make_async_copy(
            v_ref.at[:, columns(me, head)], recv.at[head, 2, rows(me), :], own_sem.at[head]
        ).start()
        pltpu.make_async_copy(
            do_ref.at[:, columns(me, head)], recv.at[head, 3, rows(me), :], own_sem.at[head]
        ).start()

        @pl.loop(1, n)
        def _(step):
            other = peer(step)
            for place, ref in ((2, v_ref), (3, do_ref)):
                remote(
                    ref.at[:, columns(other, head)], recv.at[head, place, rows(me), :],
                    in_send.at[head], in_recv.at[head], (my_dp, other),
                ).start()

    send_values(0)

    def squares(index, sums):
        cols = pl.ds(pl.multiple_of(index * LANES, LANES), LANES)
        query = q_ref[:, cols].astype(jnp.float32)
        keys = k_ref[:, cols].astype(jnp.float32)
        return sums[0] + query * query, sums[1] + keys * keys

    zero = jnp.zeros((tok, LANES), jnp.float32)
    sum_q, sum_k = lax.fori_loop(0, feature // LANES, squares, (zero, zero))
    for sums, target in ((sum_q, scale_q), (sum_k, scale_k)):
        mean = jnp.sum(sums, axis=1, keepdims=True) / feature
        target[...] = jnp.broadcast_to(lax.rsqrt(mean + EPSILON), (tok, LANES))

    def rotated(ref, gain, norm, cols):
        x = ref[:, cols].astype(jnp.float32) * norm[...] * gain[:, cols]
        turned = x * cos_ref[...] + pltpu.roll(x, HEAD_DIM // 2, 1) * sin_ref[...]
        return turned.astype(jnp.bfloat16)

    for head in range(heads):
        if head:
            send_values(head)

        @pl.loop(1, n)
        def _(step):
            other = peer(step)
            cols = columns(other, head)
            sent[head, other, 0] = rotated(q_ref, gq_ref, scale_q, cols)
            sent[head, other, 1] = rotated(k_ref, gk_ref, scale_k, cols)
            remote(
                sent.at[head, other], recv.at[head, 0:2, rows(me), :],
                in_send.at[head], in_recv.at[head], (my_dp, other),
            ).start()

        cols = columns(me, head)
        recv[head, 0, rows(me), :] = rotated(q_ref, gq_ref, scale_q, cols)
        recv[head, 1, rows(me), :] = rotated(k_ref, gk_ref, scale_k, cols)

    bounds = []
    running = len_ref[0, 0]
    for clip in range(clips):
        bounds.append(running)
        if clip + 1 < clips:
            running = running + len_ref[0, clip + 1]

    def segment(shape, dim, start):
        places = lax.broadcasted_iota(jnp.int32, shape, dim) + start
        found = jnp.zeros(shape, jnp.int32)
        for bound in bounds:
            found = found + (places >= bound).astype(jnp.int32)
        return found

    block = min(QUERY_BLOCK, tokens)

    @pl.loop(0, heads)
    def _(head):
        arrived = recv.at[head, :, pl.ds(0, (n - 1) * tok), :]
        pltpu.make_async_copy(arrived, arrived, in_recv.at[head]).wait()
        own = recv.at[head, pl.ds(2, 2), pl.ds(0, tok), :]
        pltpu.make_async_copy(own, own, own_sem.at[head]).wait()
        key_acc[...] = jnp.zeros_like(key_acc)
        value_acc[...] = jnp.zeros_like(value_acc)
        for start in range(0, tokens, block):
            low = max(0, start - reach) // LANES * LANES
            high = min(tokens, -(-(start + block + reach) // LANES) * LANES)
            query = recv[head, 0, start:start + block, :]
            keys = recv[head, 1, low:high, :]
            value_rows = recv[head, 2, low:high, :]
            cot = recv[head, 3, start:start + block, :]
            live = segment((block, 1), 0, start) == segment((1, high - low), 1, low)
            scores = jnp.where(live, dot(query, keys, 1, 1), -1e30)
            highest = jnp.max(scores, axis=1, keepdims=True)
            expon = jnp.exp((scores - highest) * scale)
            probs = expon * (1.0 / jnp.sum(expon, axis=1, keepdims=True))
            half = probs.astype(jnp.bfloat16)
            context = dot(half, value_rows, 1, 0).astype(jnp.bfloat16)
            delta = jnp.sum(
                cot.astype(jnp.float32) * context.astype(jnp.float32), axis=1, keepdims=True
            )
            dprob = dot(cot, value_rows, 1, 1)
            dscore = (probs * (dprob - delta) * scale).astype(jnp.bfloat16)
            back[head, 0, start:start + block, :] = context
            back[head, 1, start:start + block, :] = dot(dscore, keys, 1, 0).astype(jnp.bfloat16)
            key_acc[low:high, :] += dot(dscore, query, 0, 0)
            value_acc[low:high, :] += dot(half, cot, 0, 0)
        back[head, 2] = key_acc[...].astype(jnp.bfloat16)
        back[head, 3] = value_acc[...].astype(jnp.bfloat16)

        @pl.loop(1, n)
        def _(step):
            other = peer(step)
            remote(
                back.at[head, :, rows(other), :], out_ref.at[:, :, columns(me, head)],
                out_send.at[head], out_recv.at[head], (my_dp, other),
            ).start()

        out_ref[:, :, columns(me, head)] = back[head, :, rows(me), :]

    def turned_back(place, ref, norm, cols):
        grads = out_ref[place, :, cols].astype(jnp.float32)
        turned = grads * cos_ref[...] - pltpu.roll(grads, HEAD_DIM // 2, 1) * sin_ref[...]
        return turned, ref[:, cols].astype(jnp.float32) * norm[...]

    inner = (zero, zero)
    for head in range(heads):
        arrived = out_ref.at[:, :, pl.ds(0, (n - 1) * HEAD_DIM)]
        pltpu.make_async_copy(arrived, arrived, out_recv.at[head]).wait()

        def first_pass(owner, sums):
            cols = columns(owner, head)
            results = []
            for place, (ref, gain, norm) in enumerate(
                ((q_ref, gq_ref, scale_q), (k_ref, gk_ref, scale_k))
            ):
                turned, hat = turned_back(place + 1, ref, norm, cols)
                both = turned * hat
                row = place * heads + head
                part[owner, row:row + 1, :] = jnp.sum(both, axis=0, keepdims=True)
                results.append(sums[place] + both * gain[:, cols])
            return tuple(results)

        inner = lax.fori_loop(0, n, first_pass, inner)

    @pl.loop(1, n)
    def _(step):
        other = peer(step)
        remote(
            part.at[other], seq_part.at[me], gain_send.at[0], gain_recv.at[0], (my_dp, other)
        ).start()

    seq_part[me] = part[me]
    inner_q, inner_k = (
        jnp.broadcast_to(jnp.sum(sums, axis=1, keepdims=True) / feature, (tok, LANES))
        for sums in inner
    )

    def second_pass(index):
        cols = pl.ds(pl.multiple_of(index * LANES, LANES), LANES)
        for place, (ref, gain, norm, mean) in enumerate(
            ((q_ref, gq_ref, scale_q, inner_q), (k_ref, gk_ref, scale_k, inner_k))
        ):
            turned, hat = turned_back(place + 1, ref, norm, cols)
            result = norm[...] * (turned * gain[:, cols] - hat * mean)
            out_ref[place + 1, :, cols] = result.astype(jnp.bfloat16)

    pl.loop(0, feature // LANES)(second_pass)

    def wait_all(ref, count, sem):
        held = ref.at[pl.ds(0, count)]
        pltpu.make_async_copy(held, held, sem).wait()

    wait_all(seq_part, n - 1, gain_recv.at[0])
    dp_sum[...] = jnp.sum(seq_part[...], axis=0)
    for step in range(1, replicas):
        other = lax.rem(my_dp + step, replicas)
        remote(
            dp_sum, dp_part.at[my_dp], gain_send.at[1], gain_recv.at[1], (other, me)
        ).start()
    dp_part[my_dp] = dp_sum[...]
    wait_all(dp_part, replicas - 1, gain_recv.at[1])
    total[...] = jnp.sum(dp_part[...], axis=0) / replicas

    @pl.loop(1, n)
    def _(step):
        other = peer(step)
        remote(
            total, gain_ref.at[me], gain_send.at[2], gain_recv.at[2], (my_dp, other)
        ).start()

    gain_ref[me] = total[...]
    wait_all(gain_ref, n - 1, gain_recv.at[2])

    wait_all(seq_part, n - 1, gain_send.at[0])
    wait_all(dp_part, replicas - 1, gain_send.at[1])
    wait_all(seq_part, n - 1, gain_send.at[2])
    for head in range(heads):
        moved = recv.at[head, :, pl.ds(0, (n - 1) * tok), :]
        pltpu.make_async_copy(moved, moved, in_send.at[head]).wait()
        pltpu.make_async_copy(moved, moved, out_send.at[head]).wait()


def on_device(q_raw, k_raw, values, grad_out, q_gain, k_gain, lengths, positions):
    n = lax.axis_size("seq")
    replicas = lax.axis_size("dp")
    tok, feature = q_raw.shape[1:]
    heads = feature // n // HEAD_DIM
    tokens = n * tok
    reach = tokens // 3 - 1
    cosine, sine = rope_tables(positions[0], HEAD_DIM)
    sizes = (n, replicas, heads, tok, lengths.shape[1], reach)
    vmem = pl.BlockSpec(memory_space=pltpu.VMEM)
    hbm = pl.BlockSpec(memory_space=pl.ANY)
    gain_rows = (2 * heads, LANES)
    half, full = jnp.bfloat16, jnp.float32
    outs, gains = pl.pallas_call(
        functools.partial(kernel, sizes),
        out_shape=(
            jax.ShapeDtypeStruct((4, tok, feature), half),
            jax.ShapeDtypeStruct((n,) + gain_rows, full),
        ),
        in_specs=[
            pl.BlockSpec(memory_space=pltpu.SMEM), vmem, vmem, hbm, hbm, vmem, vmem, vmem, vmem,
        ],
        out_specs=(vmem, vmem),
        scratch_shapes=[
            pltpu.VMEM((heads, n, 2, tok, HEAD_DIM), half),
            pltpu.VMEM((heads, 4, tokens, HEAD_DIM), half),
            pltpu.VMEM((heads, 4, tokens, HEAD_DIM), half),
            pltpu.VMEM((tokens, HEAD_DIM), full),
            pltpu.VMEM((tokens, HEAD_DIM), full),
            pltpu.VMEM((tok, LANES), full),
            pltpu.VMEM((tok, LANES), full),
            pltpu.VMEM((n,) + gain_rows, full),
            pltpu.VMEM((n,) + gain_rows, full),
            pltpu.VMEM(gain_rows, full),
            pltpu.VMEM((replicas,) + gain_rows, full),
            pltpu.VMEM(gain_rows, full),
            pltpu.SemaphoreType.DMA((heads,)),
            pltpu.SemaphoreType.DMA((heads,)),
            pltpu.SemaphoreType.DMA((heads,)),
            pltpu.SemaphoreType.DMA((heads,)),
            pltpu.SemaphoreType.DMA((heads,)),
            pltpu.SemaphoreType.DMA((3,)),
            pltpu.SemaphoreType.DMA((3,)),
        ],
        compiler_params=pltpu.CompilerParams(
            collective_id=0, has_side_effects=True, vmem_limit_bytes=56 * 1024 * 1024
        ),
    )(
        lengths, q_raw[0], k_raw[0], values[0], grad_out[0],
        q_gain[None], k_gain[None], cosine, sine,
    )
    gains = gains.reshape(n, 2, heads * HEAD_DIM)
    return (
        outs[0][None], outs[1][None], outs[2][None], outs[3][None],
        gains[:, 0].reshape(feature), gains[:, 1].reshape(feature),
    )


def solution(mesh):
    tokens = P("dp", "seq", None)
    return jax.shard_map(
        on_device,
        mesh=mesh,
        in_specs=(tokens, tokens, tokens, tokens, P(), P(), P("dp", None), P("dp", None, "seq")),
        out_specs=(tokens, tokens, tokens, tokens, P(), P()),
        check_vma=False,
    )
```

```python
import functools

import jax
import jax.numpy as jnp
import numpy as np
from jax import lax
from jax.experimental import pallas as pl
from jax.experimental.pallas import tpu as pltpu
from jax.sharding import PartitionSpec as P

HEAD_DIM = 128
LANES = 128
QUERY_BLOCK = 256
EPSILON = 1e-06
MESH = pl.DeviceIdType.MESH


def rope_tables(position_rows, head_dim):
    half = head_dim // 2
    sixth = head_dim // 6
    first = half - 2 * sixth
    pairs = np.arange(head_dim) % half
    section = (pairs >= first).astype(np.int32) + (pairs >= first + sixth).astype(np.int32)
    begin = np.where(section == 0, 0, np.where(section == 1, first, first + sixth))
    number = np.where(section == 0, first, sixth)
    freqs = (10000.0 ** (-(pairs - begin) / number)).astype(np.float32)
    sign = np.where(np.arange(head_dim) < half, -1.0, 1.0).astype(np.float32)
    rows = position_rows.astype(jnp.float32)[:, :, None]
    chosen = jnp.where(section == 0, rows[0], jnp.where(section == 1, rows[1], rows[2]))
    angle = chosen * freqs
    return jnp.cos(angle), jnp.sin(angle) * sign


def dot(left, right, left_dim, right_dim):
    return lax.dot_general(
        left, right, (((left_dim,), (right_dim,)), ((), ())), preferred_element_type=jnp.float32
    )


def kernel(
    sizes,
    len_ref, q_ref, k_ref, v_ref, do_ref, gq_ref, gk_ref, cos_ref, sin_ref,
    out_ref, gain_ref,
    other_out, sent, recv, back, key_acc, value_acc, scale_q, scale_k,
    part, seq_part, dp_sum, dp_part, total,
    in_send, in_recv, own_sem, out_send, out_recv, gain_send, gain_recv,
    cross_in_send, cross_out_send, cross_out_recv,
):
    n, replicas, heads, tok, clips, reach, halo, padded = sizes
    members = n // 2
    half_tokens = members * tok
    window = half_tokens + halo
    feature = members * heads * HEAD_DIM
    shared = heads // 2
    me = lax.axis_index("seq")
    side = me // members
    place_in = lax.rem(me, members)
    base = side * halo
    crossing = [(d, min(tok, halo - d * tok)) for d in range(-(-halo // tok))]
    my_dp = lax.axis_index("dp")
    scale = HEAD_DIM ** (-0.5)

    def peer(step):
        return lax.rem(me + step, n)

    def member(step):
        return lax.rem(place_in + step, members)

    def device(group, index):
        return (my_dp, group * members + index)

    def columns(owner, head):
        return pl.ds(pl.multiple_of((owner * heads + head) * HEAD_DIM, HEAD_DIM), HEAD_DIM)

    def rows(owner):
        return pl.ds(pl.multiple_of(base + owner * tok, 16), tok)

    def each_crossing(act):
        for d, count in crossing:
            @pl.when(me == members - 1 - d)
            def _():
                act(1, slice(tok - count, tok), slice(halo - d * tok - count, halo - d * tok), count)

            @pl.when(me == members + d)
            def _():
                act(0, slice(0, count), slice(half_tokens + d * tok, half_tokens + d * tok + count), count)

    def remote(src, dst, send_sem, recv_sem, device):
        return pltpu.make_async_remote_copy(
            src_ref=src, dst_ref=dst, send_sem=send_sem, recv_sem=recv_sem,
            device_id=device, device_id_type=MESH,
        )

    barrier = pltpu.get_barrier_semaphore()
    for step in range(1, n):
        pl.semaphore_signal(barrier, inc=1, device_id=(my_dp, peer(step)), device_id_type=MESH)
    for step in range(1, replicas):
        other = lax.rem(my_dp + step, replicas)
        pl.semaphore_signal(barrier, inc=1, device_id=(other, me), device_id_type=MESH)
    pl.semaphore_wait(barrier, n - 1 + replicas - 1)

    def send_values(head):
        cols = columns(place_in, head)
        for place, ref in ((2, v_ref), (3, do_ref)):
            pltpu.make_async_copy(
                ref.at[:, cols], recv.at[head, place, rows(place_in), :], own_sem.at[head]
            ).start()

        def cross(group, source, target, count):
            @pl.loop(0, members)
            def _(step):
                other = member(step)
                for place, ref in ((2, v_ref), (3, do_ref)):
                    remote(
                        ref.at[source, columns(other, head)], recv.at[head, place, target, :],
                        cross_in_send.at[head], in_recv.at[head], device(group, other),
                    ).start()

        each_crossing(cross)

        @pl.loop(1, members)
        def _(step):
            other = member(step)
            for place, ref in ((2, v_ref), (3, do_ref)):
                remote(
                    ref.at[:, columns(other, head)], recv.at[head, place, rows(place_in), :],
                    in_send.at[head], in_recv.at[head], device(side, other),
                ).start()

    send_values(0)

    def squares(index, sums):
        cols = pl.ds(pl.multiple_of(index * LANES, LANES), LANES)
        query = q_ref[:, cols].astype(jnp.float32)
        keys = k_ref[:, cols].astype(jnp.float32)
        return sums[0] + query * query, sums[1] + keys * keys

    zero = jnp.zeros((tok, LANES), jnp.float32)
    sum_q, sum_k = lax.fori_loop(0, feature // LANES, squares, (zero, zero))
    for sums, target in ((sum_q, scale_q), (sum_k, scale_k)):
        mean = jnp.sum(sums, axis=1, keepdims=True) / feature
        target[...] = jnp.broadcast_to(lax.rsqrt(mean + EPSILON), (tok, LANES))

    def rotated(ref, gain, norm, cols):
        x = ref[:, cols].astype(jnp.float32) * norm[...] * gain[:, cols]
        turned = x * cos_ref[...] + pltpu.roll(x, HEAD_DIM // 2, 1) * sin_ref[...]
        return turned.astype(jnp.bfloat16)

    @pl.loop(0, heads)
    def _(head):
        @pl.when(head > 0)
        def _():
            send_values(head)

        @pl.loop(1, members)
        def _(step):
            other = member(step)
            cols = columns(other, head)
            sent[head, other, 0] = rotated(q_ref, gq_ref, scale_q, cols)
            sent[head, other, 1] = rotated(k_ref, gk_ref, scale_k, cols)
            remote(
                sent.at[head, other], recv.at[head, 0:2, rows(place_in), :],
                in_send.at[head], in_recv.at[head], device(side, other),
            ).start()

        cols = columns(place_in, head)
        for place, (ref, gain, norm) in enumerate(((q_ref, gq_ref, scale_q), (k_ref, gk_ref, scale_k))):
            moved = rotated(ref, gain, norm, cols)
            sent[head, place_in, place] = moved
            recv[head, place, rows(place_in), :] = moved

        def cross(group, source, target, count):
            @pl.loop(0, members)
            def _(step):
                other = member(step)
                remote(
                    sent.at[head, other, :, source, :], recv.at[head, 0:2, target, :],
                    cross_in_send.at[head], in_recv.at[head], device(group, other),
                ).start()

        each_crossing(cross)

    bounds = []
    running = len_ref[0, 0]
    for clip in range(clips):
        bounds.append(running)
        if clip + 1 < clips:
            running = running + len_ref[0, clip + 1]

    first, last = jnp.int32(0), jnp.int32(2 * half_tokens)
    for bound in bounds:
        first = jnp.maximum(first, jnp.where(bound <= half_tokens, bound, 0))
        last = jnp.minimum(last, jnp.where(bound > half_tokens, bound, 2 * half_tokens))
    low_owns = last - half_tokens <= half_tokens - first
    low_edge = jnp.where(low_owns, half_tokens, first)
    high_edge = jnp.where(low_owns, last, half_tokens)
    tail = padded - window
    if tail:
        @pl.loop(0, heads)
        def _(head):
            recv[head, :, window:padded, :] = jnp.zeros((4, tail, HEAD_DIM), jnp.bfloat16)

    def segment(shape, dim, start):
        inside = lax.broadcasted_iota(jnp.int32, shape, dim) + start
        places = inside + side * (half_tokens - halo)
        found = jnp.zeros(shape, jnp.int32)
        for bound in bounds:
            found = found + (places >= bound).astype(jnp.int32)
        return jnp.where(inside < window, found, -1)

    @pl.loop(0, heads)
    def _(head):
        arrived = recv.at[head, :, pl.ds(0, (members - 1) * tok + halo), :]
        pltpu.make_async_copy(arrived, arrived, in_recv.at[head]).wait()
        own = recv.at[head, pl.ds(2, 2), pl.ds(0, tok), :]
        pltpu.make_async_copy(own, own, own_sem.at[head]).wait()
        key_acc[...] = jnp.zeros_like(key_acc)
        value_acc[...] = jnp.zeros_like(value_acc)
        for start in range(0, window, QUERY_BLOCK):
            block = min(QUERY_BLOCK, window - start)
            low = max(0, start - reach) // LANES * LANES
            high = min(padded, -(-(start + block + reach) // LANES) * LANES)
            query = recv[head, 0, start:start + block, :]
            keys = recv[head, 1, low:high, :]
            value_rows = recv[head, 2, low:high, :]
            cot = recv[head, 3, start:start + block, :]
            live = segment((block, 1), 0, start) == segment((1, high - low), 1, low)
            scores = jnp.where(live, dot(query, keys, 1, 1), -1e30)
            highest = jnp.max(scores, axis=1, keepdims=True)
            expon = jnp.exp((scores - highest) * scale)
            probs = expon * (1.0 / jnp.sum(expon, axis=1, keepdims=True))
            half = probs.astype(jnp.bfloat16)
            context = dot(half, value_rows, 1, 0).astype(jnp.bfloat16)
            delta = jnp.sum(
                cot.astype(jnp.float32) * context.astype(jnp.float32), axis=1, keepdims=True
            )
            dprob = dot(cot, value_rows, 1, 1)
            dscore = (probs * (dprob - delta) * scale).astype(jnp.bfloat16)
            back[head, 0, start:start + block, :] = context
            back[head, 1, start:start + block, :] = dot(dscore, keys, 1, 0).astype(jnp.bfloat16)
            key_acc[low:high, :] += dot(dscore, query, 0, 0)
            value_acc[low:high, :] += dot(half, cot, 0, 0)
        back[head, 2] = key_acc[0:window, :].astype(jnp.bfloat16)
        back[head, 3] = value_acc[0:window, :].astype(jnp.bfloat16)
        cols = columns(place_in, head)
        for d, count in crossing:
            @pl.when(side == 0)
            def _():
                edge = half_tokens + d * tok
                remote(
                    back.at[head, :, edge:edge + count, :], other_out.at[:, 0:count, cols],
                    cross_out_send.at[head], cross_out_recv.at[head], device(1, d),
                ).start()

            @pl.when(side == 1)
            def _():
                edge = halo - d * tok - count
                remote(
                    back.at[head, :, edge:edge + count, :], other_out.at[:, tok - count:tok, cols],
                    cross_out_send.at[head], cross_out_recv.at[head], device(0, members - 1 - d),
                ).start()

        @pl.loop(1, members)
        def _(step):
            other = member(step)
            remote(
                back.at[head, :, rows(other), :], out_ref.at[:, :, cols],
                out_send.at[head], out_recv.at[head], device(side, other),
            ).start()

        out_ref[:, :, cols] = back[head, :, rows(place_in), :]

    def turned_back(place, ref, norm, cols):
        grads = out_ref[place, :, cols].astype(jnp.float32)
        turned = grads * cos_ref[...] - pltpu.roll(grads, HEAD_DIM // 2, 1) * sin_ref[...]
        return turned, ref[:, cols].astype(jnp.float32) * norm[...]

    inner = (zero, zero)
    for head in range(heads):
        arrived = out_ref.at[:, :, pl.ds(0, (members - 1) * HEAD_DIM)]
        pltpu.make_async_copy(arrived, arrived, out_recv.at[head]).wait()

        def merge(group, source, target, count):
            crossed = other_out.at[:, source, pl.ds(0, members * HEAD_DIM)]
            pltpu.make_async_copy(crossed, crossed, cross_out_recv.at[head]).wait()
            places = lax.broadcasted_iota(jnp.int32, (count, HEAD_DIM), 0) + me * tok + source.start
            outside = (places >= low_edge) if group == 1 else (places < high_edge)

            @pl.loop(0, members)
            def _(owner):
                cols = columns(owner, head)
                for place in range(4):
                    out_ref[place, source, cols] = jnp.where(
                        outside, other_out[place, source, cols], out_ref[place, source, cols]
                    )

        each_crossing(merge)

        def first_pass(owner, sums):
            cols = columns(owner, head)
            results = []
            for place, (ref, gain, norm) in enumerate(
                ((q_ref, gq_ref, scale_q), (k_ref, gk_ref, scale_k))
            ):
                turned, hat = turned_back(place + 1, ref, norm, cols)
                both = turned * hat
                row = place * shared + head % shared
                part[owner * 2 + head // shared, row:row + 1, :] = jnp.sum(both, axis=0, keepdims=True)
                results.append(sums[place] + both * gain[:, cols])
            return tuple(results)

        inner = lax.fori_loop(0, members, first_pass, inner)

    @pl.loop(1, n)
    def _(step):
        other = peer(step)
        remote(
            part.at[other], seq_part.at[me], gain_send.at[0], gain_recv.at[0], (my_dp, other)
        ).start()

    seq_part[me] = part[me]
    inner_q, inner_k = (
        jnp.broadcast_to(jnp.sum(sums, axis=1, keepdims=True) / feature, (tok, LANES))
        for sums in inner
    )

    def second_pass(index):
        cols = pl.ds(pl.multiple_of(index * LANES, LANES), LANES)
        for place, (ref, gain, norm, mean) in enumerate(
            ((q_ref, gq_ref, scale_q, inner_q), (k_ref, gk_ref, scale_k, inner_k))
        ):
            turned, hat = turned_back(place + 1, ref, norm, cols)
            result = norm[...] * (turned * gain[:, cols] - hat * mean)
            out_ref[place + 1, :, cols] = result.astype(jnp.bfloat16)

    pl.loop(0, feature // LANES)(second_pass)

    def wait_all(ref, count, sem):
        held = ref.at[pl.ds(0, count)]
        pltpu.make_async_copy(held, held, sem).wait()

    wait_all(seq_part, n - 1, gain_recv.at[0])
    dp_sum[...] = jnp.sum(seq_part[...], axis=0)
    for step in range(1, replicas):
        other = lax.rem(my_dp + step, replicas)
        remote(
            dp_sum, dp_part.at[my_dp], gain_send.at[1], gain_recv.at[1], (other, me)
        ).start()
    dp_part[my_dp] = dp_sum[...]
    wait_all(dp_part, replicas - 1, gain_recv.at[1])
    total[...] = jnp.sum(dp_part[...], axis=0) / replicas

    @pl.loop(1, n)
    def _(step):
        other = peer(step)
        remote(
            total, gain_ref.at[me], gain_send.at[2], gain_recv.at[2], (my_dp, other)
        ).start()

    gain_ref[me] = total[...]
    wait_all(gain_ref, n - 1, gain_recv.at[2])

    wait_all(seq_part, n - 1, gain_send.at[0])
    wait_all(dp_part, replicas - 1, gain_send.at[1])
    wait_all(seq_part, n - 1, gain_send.at[2])
    for head in range(heads):
        moved = recv.at[head, :, pl.ds(0, (members - 1) * tok), :]
        pltpu.make_async_copy(moved, moved, in_send.at[head]).wait()
        pltpu.make_async_copy(moved, moved, out_send.at[head]).wait()
        moved = recv.at[head, :, pl.ds(0, halo), :]
        pltpu.make_async_copy(moved, moved, cross_out_send.at[head]).wait()

        def drain(group, source, target, count):
            moved = other_out.at[:, source, pl.ds(0, members * HEAD_DIM)]
            pltpu.make_async_copy(moved, moved, cross_in_send.at[head]).wait()

        each_crossing(drain)


def on_device(q_raw, k_raw, values, grad_out, q_gain, k_gain, lengths, positions):
    n = lax.axis_size("seq")
    replicas = lax.axis_size("dp")
    tok, feature = q_raw.shape[1:]
    shared = feature // n // HEAD_DIM
    heads = 2 * shared
    tokens = n * tok
    reach = tokens // 3 - 1
    halo = -(-((reach + 1) // 2) // 16) * 16
    window = tokens // 2 + halo
    padded = -(-window // LANES) * LANES
    cosine, sine = rope_tables(positions[0], HEAD_DIM)
    sizes = (n, replicas, heads, tok, lengths.shape[1], reach, halo, padded)
    vmem = pl.BlockSpec(memory_space=pltpu.VMEM)
    hbm = pl.BlockSpec(memory_space=pl.ANY)
    gain_rows = (2 * shared, LANES)
    half, full = jnp.bfloat16, jnp.float32
    outs, gains = pl.pallas_call(
        functools.partial(kernel, sizes),
        out_shape=(
            jax.ShapeDtypeStruct((4, tok, feature), half),
            jax.ShapeDtypeStruct((n,) + gain_rows, full),
        ),
        in_specs=[
            pl.BlockSpec(memory_space=pltpu.SMEM), vmem, vmem, hbm, hbm, vmem, vmem, vmem, vmem,
        ],
        out_specs=(vmem, vmem),
        scratch_shapes=[
            pltpu.VMEM((4, tok, feature), half),
            pltpu.VMEM((heads, n // 2, 2, tok, HEAD_DIM), half),
            pltpu.VMEM((heads, 4, padded, HEAD_DIM), half),
            pltpu.VMEM((heads, 4, window, HEAD_DIM), half),
            pltpu.VMEM((padded, HEAD_DIM), full),
            pltpu.VMEM((padded, HEAD_DIM), full),
            pltpu.VMEM((tok, LANES), full),
            pltpu.VMEM((tok, LANES), full),
            pltpu.VMEM((n,) + gain_rows, full),
            pltpu.VMEM((n,) + gain_rows, full),
            pltpu.VMEM(gain_rows, full),
            pltpu.VMEM((replicas,) + gain_rows, full),
            pltpu.VMEM(gain_rows, full),
            pltpu.SemaphoreType.DMA((heads,)),
            pltpu.SemaphoreType.DMA((heads,)),
            pltpu.SemaphoreType.DMA((heads,)),
            pltpu.SemaphoreType.DMA((heads,)),
            pltpu.SemaphoreType.DMA((heads,)),
            pltpu.SemaphoreType.DMA((3,)),
            pltpu.SemaphoreType.DMA((3,)),
            pltpu.SemaphoreType.DMA((heads,)),
            pltpu.SemaphoreType.DMA((heads,)),
            pltpu.SemaphoreType.DMA((heads,)),
        ],
        compiler_params=pltpu.CompilerParams(
            collective_id=0, has_side_effects=True, vmem_limit_bytes=56 * 1024 * 1024
        ),
    )(
        lengths, q_raw[0], k_raw[0], values[0], grad_out[0],
        q_gain[None], k_gain[None], cosine, sine,
    )
    gains = gains.reshape(n, 2, shared * HEAD_DIM)
    return (
        outs[0][None], outs[1][None], outs[2][None], outs[3][None],
        gains[:, 0].reshape(feature), gains[:, 1].reshape(feature),
    )


def solution(mesh):
    tokens = P("dp", "seq", None)
    return jax.shard_map(
        on_device,
        mesh=mesh,
        in_specs=(tokens, tokens, tokens, tokens, P(), P(), P("dp", None), P("dp", None, "seq")),
        out_specs=(tokens, tokens, tokens, tokens, P(), P()),
        check_vma=False,
    )
```

```python
import functools

import jax
import jax.numpy as jnp
import numpy as np
from jax import lax
from jax.experimental import pallas as pl
from jax.experimental.pallas import tpu as pltpu
from jax.sharding import PartitionSpec as P

HEAD_DIM = 128
LANES = 128
QUERY_BLOCK = 256
GROUPS = 4
ATTEND_LAG = 2
DISTRIBUTE_LAG = 2
EPSILON = 1e-06
MESH = pl.DeviceIdType.MESH


def rope_tables(position_rows, head_dim):
    half = head_dim // 2
    sixth = head_dim // 6
    first = half - 2 * sixth
    pairs = np.arange(head_dim) % half
    section = (pairs >= first).astype(np.int32) + (pairs >= first + sixth).astype(np.int32)
    begin = np.where(section == 0, 0, np.where(section == 1, first, first + sixth))
    number = np.where(section == 0, first, sixth)
    freqs = (10000.0 ** (-(pairs - begin) / number)).astype(np.float32)
    sign = np.where(np.arange(head_dim) < half, -1.0, 1.0).astype(np.float32)
    rows = position_rows.astype(jnp.float32)[:, :, None]
    chosen = jnp.where(section == 0, rows[0], jnp.where(section == 1, rows[1], rows[2]))
    angle = chosen * freqs
    return jnp.cos(angle), jnp.sin(angle) * sign


def dot(left, right, left_dim, right_dim):
    return lax.dot_general(
        left, right, (((left_dim,), (right_dim,)), ((), ())), preferred_element_type=jnp.float32
    )


def kernel(
    sizes,
    len_ref, q_ref, k_ref, v_ref, do_ref, gq_ref, gk_ref, cos_ref, sin_ref,
    out_ref, gain_ref,
    beside, sent, recv, back, key_acc, value_acc, scale_q, scale_k,
    part, seq_part, dp_sum, dp_part, total,
    in_send, in_recv, own_sem, out_send, out_recv, gain_send, gain_recv,
    halo_send, halo_recv, beside_send, beside_recv,
):
    n, replicas, heads, tok, clips, reach, halo, padded = sizes
    members = n // GROUPS
    group_tokens = members * tok
    group_end = halo + group_tokens
    window = group_end + halo
    feature = members * heads * HEAD_DIM
    ratio = GROUPS
    shared = heads // ratio
    me = lax.axis_index("seq")
    side = me // members
    place_in = lax.rem(me, members)
    my_dp = lax.axis_index("dp")
    scale = HEAD_DIM ** (-0.5)

    def peer(step):
        return lax.rem(me + step, n)

    def member(step):
        return lax.rem(place_in + step, members)

    def device(group, index):
        return (my_dp, group * members + index)

    def columns(owner, head):
        return pl.ds(pl.multiple_of((owner * heads + head) * HEAD_DIM, HEAD_DIM), HEAD_DIM)

    def rows(owner):
        return pl.ds(pl.multiple_of(halo + owner * tok, 16), tok)

    def each_side(act):
        @pl.when(side > 0)
        def _():
            act(0, side - 1)

        @pl.when(side < GROUPS - 1)
        def _():
            act(1, side + 1)

    def remote(src, dst, send_sem, recv_sem, device):
        return pltpu.make_async_remote_copy(
            src_ref=src, dst_ref=dst, send_sem=send_sem, recv_sem=recv_sem,
            device_id=device, device_id_type=MESH,
        )

    barrier = pltpu.get_barrier_semaphore()
    for step in range(1, n):
        pl.semaphore_signal(barrier, inc=1, device_id=(my_dp, peer(step)), device_id_type=MESH)
    for step in range(1, replicas):
        other = lax.rem(my_dp + step, replicas)
        pl.semaphore_signal(barrier, inc=1, device_id=(other, me), device_id_type=MESH)
    pl.semaphore_wait(barrier, n - 1 + replicas - 1)

    def send_values(head):
        cols = columns(place_in, head)
        for place, ref in ((2, v_ref), (3, do_ref)):
            pltpu.make_async_copy(
                ref.at[:, cols], recv.at[head, place, rows(place_in), :], own_sem.at[head]
            ).start()

        @pl.loop(1, members)
        def _(step):
            other = member(step)
            for place, ref in ((2, v_ref), (3, do_ref)):
                remote(
                    ref.at[:, columns(other, head)], recv.at[head, place, rows(place_in), :],
                    in_send.at[head], in_recv.at[head], device(side, other),
                ).start()

    send_values(0)

    def squares(index, sums):
        cols = pl.ds(pl.multiple_of(index * LANES, LANES), LANES)
        query = q_ref[:, cols].astype(jnp.float32)
        keys = k_ref[:, cols].astype(jnp.float32)
        return sums[0] + query * query, sums[1] + keys * keys

    zero = jnp.zeros((tok, LANES), jnp.float32)
    sum_q, sum_k = lax.fori_loop(0, feature // LANES, squares, (zero, zero))
    for sums, target in ((sum_q, scale_q), (sum_k, scale_k)):
        mean = jnp.sum(sums, axis=1, keepdims=True) / feature
        target[...] = jnp.broadcast_to(lax.rsqrt(mean + EPSILON), (tok, LANES))

    def rotated(ref, gain, norm, cols):
        x = ref[:, cols].astype(jnp.float32) * norm[...] * gain[:, cols]
        turned = x * cos_ref[...] + pltpu.roll(x, HEAD_DIM // 2, 1) * sin_ref[...]
        return turned.astype(jnp.bfloat16)

    @pl.loop(0, heads)
    def _(head):
        @pl.when(head > 0)
        def _():
            send_values(head)

        @pl.loop(1, members)
        def _(step):
            other = member(step)
            cols = columns(other, head)
            sent[head, other, 0] = rotated(q_ref, gq_ref, scale_q, cols)
            sent[head, other, 1] = rotated(k_ref, gk_ref, scale_k, cols)
            remote(
                sent.at[head, other], recv.at[head, 0:2, rows(place_in), :],
                in_send.at[head], in_recv.at[head], device(side, other),
            ).start()

        cols = columns(place_in, head)
        for place, (ref, gain, norm) in enumerate(((q_ref, gq_ref, scale_q), (k_ref, gk_ref, scale_k))):
            recv[head, place, rows(place_in), :] = rotated(ref, gain, norm, cols)

    bounds = []
    running = len_ref[0, 0]
    for clip in range(clips):
        bounds.append(running)
        if clip + 1 < clips:
            running = running + len_ref[0, clip + 1]

    def edges(middle):
        first, last = jnp.int32(0), jnp.int32(n * tok)
        for bound in bounds:
            first = jnp.maximum(first, jnp.where(bound <= middle, bound, 0))
            last = jnp.minimum(last, jnp.where(bound > middle, bound, n * tok))
        low_owns = last - middle <= middle - first
        return jnp.where(low_owns, middle, first), jnp.where(low_owns, last, middle)

    token_start = side * group_tokens
    high_edge = edges(token_start)[1]
    low_edge = edges(token_start + group_tokens)[0]

    def clear(begin, end):
        @pl.loop(0, heads)
        def _(head):
            recv[head, :, begin:end, :] = jnp.zeros((4, end - begin, HEAD_DIM), jnp.bfloat16)

    if padded > window:
        clear(window, padded)

    @pl.when(side == 0)
    def _():
        clear(0, halo)

    @pl.when(side == GROUPS - 1)
    def _():
        clear(group_end, window)

    def segment(shape, dim, start):
        inside = lax.broadcasted_iota(jnp.int32, shape, dim) + start
        places = inside + (token_start - halo)
        found = jnp.zeros(shape, jnp.int32)
        for bound in bounds:
            found = found + (places >= bound).astype(jnp.int32)
        valid = (inside < window) & (places >= 0) & (places < n * tok)
        return jnp.where(valid, found, -1)

    group_rows = ((halo, halo + halo), (group_end - halo, group_end))
    halo_rows = ((0, halo), (group_end, window))

    def relay(head):
        arrived = recv.at[head, :, pl.ds(0, (members - 1) * tok), :]
        pltpu.make_async_copy(arrived, arrived, in_recv.at[head]).wait()
        own = recv.at[head, pl.ds(2, 2), pl.ds(0, tok), :]
        pltpu.make_async_copy(own, own, own_sem.at[head]).wait()

        def act(which, group):
            source, target = group_rows[which], halo_rows[1 - which]
            remote(
                recv.at[head, :, source[0]:source[1], :], recv.at[head, :, target[0]:target[1], :],
                halo_send.at[which, head], halo_recv.at[1 - which, head], device(group, place_in),
            ).start()

        each_side(act)

    def attend(head):
        def arrive(which, group):
            target = halo_rows[which]
            held = recv.at[head, :, target[0]:target[1], :]
            pltpu.make_async_copy(held, held, halo_recv.at[which, head]).wait()

        each_side(arrive)
        key_acc[...] = jnp.zeros_like(key_acc)
        value_acc[...] = jnp.zeros_like(value_acc)
        for start in range(0, window, QUERY_BLOCK):
            block = min(QUERY_BLOCK, window - start)
            low = max(0, start - reach) // LANES * LANES
            high = min(padded, -(-(start + block + reach) // LANES) * LANES)
            query = recv[head, 0, start:start + block, :]
            keys = recv[head, 1, low:high, :]
            value_rows = recv[head, 2, low:high, :]
            cot = recv[head, 3, start:start + block, :]
            live = segment((block, 1), 0, start) == segment((1, high - low), 1, low)
            scores = jnp.where(live, dot(query, keys, 1, 1), -1e30)
            highest = jnp.max(scores, axis=1, keepdims=True)
            expon = jnp.exp((scores - highest) * scale)
            probs = expon * (1.0 / jnp.sum(expon, axis=1, keepdims=True))
            half = probs.astype(jnp.bfloat16)
            context = dot(half, value_rows, 1, 0).astype(jnp.bfloat16)
            delta = jnp.sum(
                cot.astype(jnp.float32) * context.astype(jnp.float32), axis=1, keepdims=True
            )
            dprob = dot(cot, value_rows, 1, 1)
            dscore = (probs * (dprob - delta) * scale).astype(jnp.bfloat16)
            back[head, 0, start:start + block, :] = context
            back[head, 1, start:start + block, :] = dot(dscore, keys, 1, 0).astype(jnp.bfloat16)
            key_acc[low:high, :] += dot(dscore, query, 0, 0)
            value_acc[low:high, :] += dot(half, cot, 0, 0)
        back[head, 2] = key_acc[0:window, :].astype(jnp.bfloat16)
        back[head, 3] = value_acc[0:window, :].astype(jnp.bfloat16)

        def act(which, group):
            source = halo_rows[which]
            remote(
                back.at[head, :, source[0]:source[1], :], beside.at[head, 1 - which],
                beside_send.at[which, head], beside_recv.at[1 - which, head],
                device(group, place_in),
            ).start()

        each_side(act)

    def distribute(head):
        def merge(which, group):
            held = beside.at[head, which]
            pltpu.make_async_copy(held, held, beside_recv.at[which, head]).wait()
            begin, end = group_rows[which]
            places = lax.broadcasted_iota(jnp.int32, (halo, HEAD_DIM), 0) + (
                token_start + begin - halo
            )
            outside = (places >= low_edge) if which else (places < high_edge)
            for place in range(4):
                back[head, place, begin:end, :] = jnp.where(
                    outside, beside[head, which, place], back[head, place, begin:end, :]
                )

        each_side(merge)
        cols = columns(place_in, head)

        @pl.loop(1, members)
        def _(step):
            other = member(step)
            remote(
                back.at[head, :, rows(other), :], out_ref.at[:, :, cols],
                out_send.at[head], out_recv.at[head], device(side, other),
            ).start()

        out_ref[:, :, cols] = back[head, :, rows(place_in), :]

    @pl.loop(0, heads + ATTEND_LAG + DISTRIBUTE_LAG)
    def _(step):
        @pl.when(step < heads)
        def _():
            relay(step)

        @pl.when((step >= ATTEND_LAG) & (step < heads + ATTEND_LAG))
        def _():
            attend(step - ATTEND_LAG)

        @pl.when(step >= ATTEND_LAG + DISTRIBUTE_LAG)
        def _():
            distribute(step - ATTEND_LAG - DISTRIBUTE_LAG)

    def turned_back(place, ref, norm, cols):
        grads = out_ref[place, :, cols].astype(jnp.float32)
        turned = grads * cos_ref[...] - pltpu.roll(grads, HEAD_DIM // 2, 1) * sin_ref[...]
        return turned, ref[:, cols].astype(jnp.float32) * norm[...]

    inner = (zero, zero)
    for head in range(heads):
        arrived = out_ref.at[:, :, pl.ds(0, (members - 1) * HEAD_DIM)]
        pltpu.make_async_copy(arrived, arrived, out_recv.at[head]).wait()

        def first_pass(owner, sums):
            cols = columns(owner, head)
            results = []
            for place, (ref, gain, norm) in enumerate(
                ((q_ref, gq_ref, scale_q), (k_ref, gk_ref, scale_k))
            ):
                turned, hat = turned_back(place + 1, ref, norm, cols)
                both = turned * hat
                row = place * shared + head % shared
                part[owner * ratio + head // shared, row:row + 1, :] = jnp.sum(both, axis=0, keepdims=True)
                results.append(sums[place] + both * gain[:, cols])
            return tuple(results)

        inner = lax.fori_loop(0, members, first_pass, inner)

    @pl.loop(1, n)
    def _(step):
        other = peer(step)
        remote(
            part.at[other], seq_part.at[me], gain_send.at[0], gain_recv.at[0], (my_dp, other)
        ).start()

    seq_part[me] = part[me]
    inner_q, inner_k = (
        jnp.broadcast_to(jnp.sum(sums, axis=1, keepdims=True) / feature, (tok, LANES))
        for sums in inner
    )

    def second_pass(index):
        cols = pl.ds(pl.multiple_of(index * LANES, LANES), LANES)
        for place, (ref, gain, norm, mean) in enumerate(
            ((q_ref, gq_ref, scale_q, inner_q), (k_ref, gk_ref, scale_k, inner_k))
        ):
            turned, hat = turned_back(place + 1, ref, norm, cols)
            result = norm[...] * (turned * gain[:, cols] - hat * mean)
            out_ref[place + 1, :, cols] = result.astype(jnp.bfloat16)

    pl.loop(0, feature // LANES)(second_pass)

    def wait_all(ref, count, sem):
        held = ref.at[pl.ds(0, count)]
        pltpu.make_async_copy(held, held, sem).wait()

    wait_all(seq_part, n - 1, gain_recv.at[0])
    dp_sum[...] = jnp.sum(seq_part[...], axis=0)
    for step in range(1, replicas):
        other = lax.rem(my_dp + step, replicas)
        remote(
            dp_sum, dp_part.at[my_dp], gain_send.at[1], gain_recv.at[1], (other, me)
        ).start()
    dp_part[my_dp] = dp_sum[...]
    wait_all(dp_part, replicas - 1, gain_recv.at[1])
    total[...] = jnp.sum(dp_part[...], axis=0) / replicas

    @pl.loop(1, n)
    def _(step):
        other = peer(step)
        remote(
            total, gain_ref.at[me], gain_send.at[2], gain_recv.at[2], (my_dp, other)
        ).start()

    gain_ref[me] = total[...]
    wait_all(gain_ref, n - 1, gain_recv.at[2])

    wait_all(seq_part, n - 1, gain_send.at[0])
    wait_all(dp_part, replicas - 1, gain_send.at[1])
    wait_all(seq_part, n - 1, gain_send.at[2])
    for head in range(heads):
        moved = recv.at[head, :, pl.ds(0, (members - 1) * tok), :]
        pltpu.make_async_copy(moved, moved, in_send.at[head]).wait()
        pltpu.make_async_copy(moved, moved, out_send.at[head]).wait()

        def drain(which, group):
            held = beside.at[head, which]
            pltpu.make_async_copy(held, held, halo_send.at[which, head]).wait()
            pltpu.make_async_copy(held, held, beside_send.at[which, head]).wait()

        each_side(drain)


def on_device(q_raw, k_raw, values, grad_out, q_gain, k_gain, lengths, positions):
    n = lax.axis_size("seq")
    replicas = lax.axis_size("dp")
    tok, feature = q_raw.shape[1:]
    shared = feature // n // HEAD_DIM
    heads = GROUPS * shared
    tokens = n * tok
    reach = tokens // 3 - 1
    halo = -(-((reach + 1) // 2) // 16) * 16
    window = tokens // GROUPS + 2 * halo
    padded = -(-window // LANES) * LANES
    cosine, sine = rope_tables(positions[0], HEAD_DIM)
    sizes = (n, replicas, heads, tok, lengths.shape[1], reach, halo, padded)
    vmem = pl.BlockSpec(memory_space=pltpu.VMEM)
    hbm = pl.BlockSpec(memory_space=pl.ANY)
    gain_rows = (2 * shared, LANES)
    half, full = jnp.bfloat16, jnp.float32
    outs, gains = pl.pallas_call(
        functools.partial(kernel, sizes),
        out_shape=(
            jax.ShapeDtypeStruct((4, tok, feature), half),
            jax.ShapeDtypeStruct((n,) + gain_rows, full),
        ),
        in_specs=[
            pl.BlockSpec(memory_space=pltpu.SMEM), vmem, vmem, hbm, hbm, vmem, vmem, vmem, vmem,
        ],
        out_specs=(vmem, vmem),
        scratch_shapes=[
            pltpu.VMEM((heads, 2, 4, halo, HEAD_DIM), half),
            pltpu.VMEM((heads, n // GROUPS, 2, tok, HEAD_DIM), half),
            pltpu.VMEM((heads, 4, padded, HEAD_DIM), half),
            pltpu.VMEM((heads, 4, window, HEAD_DIM), half),
            pltpu.VMEM((padded, HEAD_DIM), full),
            pltpu.VMEM((padded, HEAD_DIM), full),
            pltpu.VMEM((tok, LANES), full),
            pltpu.VMEM((tok, LANES), full),
            pltpu.VMEM((n,) + gain_rows, full),
            pltpu.VMEM((n,) + gain_rows, full),
            pltpu.VMEM(gain_rows, full),
            pltpu.VMEM((replicas,) + gain_rows, full),
            pltpu.VMEM(gain_rows, full),
            pltpu.SemaphoreType.DMA((heads,)),
            pltpu.SemaphoreType.DMA((heads,)),
            pltpu.SemaphoreType.DMA((heads,)),
            pltpu.SemaphoreType.DMA((heads,)),
            pltpu.SemaphoreType.DMA((heads,)),
            pltpu.SemaphoreType.DMA((3,)),
            pltpu.SemaphoreType.DMA((3,)),
            pltpu.SemaphoreType.DMA((2, heads)),
            pltpu.SemaphoreType.DMA((2, heads)),
            pltpu.SemaphoreType.DMA((2, heads)),
            pltpu.SemaphoreType.DMA((2, heads)),
        ],
        compiler_params=pltpu.CompilerParams(
            collective_id=0, has_side_effects=True, vmem_limit_bytes=56 * 1024 * 1024
        ),
    )(
        lengths, q_raw[0], k_raw[0], values[0], grad_out[0],
        q_gain[None], k_gain[None], cosine, sine,
    )
    gains = gains.reshape(n, 2, shared * HEAD_DIM)
    return (
        outs[0][None], outs[1][None], outs[2][None], outs[3][None],
        gains[:, 0].reshape(feature), gains[:, 1].reshape(feature),
    )


def solution(mesh):
    tokens = P("dp", "seq", None)
    return jax.shard_map(
        on_device,
        mesh=mesh,
        in_specs=(tokens, tokens, tokens, tokens, P(), P(), P("dp", None), P("dp", None, "seq")),
        out_specs=(tokens, tokens, tokens, tokens, P(), P()),
        check_vma=False,
    )
```
